256 devices in a mesh: dp: 32 (over z, y_hi, core), mp: 8 (over x, y_lo).
Axes of the slice: x: 4, y: 4 (y_hi: 2, y_lo: 2; y = y_hi * 2 + y_lo), z: 8, core: 2. Of those that a mesh axis runs over, the one named last changes fastest.
Arguments:
- token_ids: int32 [128, 64], P(None, 'dp'), may hold values from 0 to 1023
- fanout: int32 [128, 16], replicated, may hold values from 1 to 16
- table_of_column: int32 [64], P('dp'), may hold values from 0 to 15
- embed_table: bfloat16 [64, 1024, 1024], P('dp', 'mp'), may hold values from -35 to 35
- start_vector: bfloat16 [1024], replicated, may hold values from -6 to 6
- gain_attn: bfloat16 [1024], replicated, may hold values from 0.25 to 1.75
- gain_mlp: bfloat16 [1024], replicated, may hold values from 0.25 to 1.75
- gain_final: bfloat16 [1024], replicated, may hold values from 0.25 to 1.75
- w_qkv: bfloat16 [1024, 3, 1024], P(None, None, 'mp'), may hold values from -8 to 8
- w_out: bfloat16 [1024, 1024], P(None, 'mp'), may hold values from -0.1875 to 0.1875
- w_gate: bfloat16 [1024, 4096], P(None, 'mp'), may hold values from -0.1875 to 0.1875
- w_up: bfloat16 [1024, 4096], P(None, 'mp'), may hold values from -0.1875 to 0.1875
- w_down: bfloat16 [1024, 4096], P(None, 'mp'), may hold values from -0.09375 to 0.09375
Outputs:
- nll: float32 [128, 64], P(None, 'dp')
- grad_table: float32 [64, 1024, 1024], P('dp', 'mp')
- grad_qkv: float32 [1024, 3, 1024], P('dp', None, 'mp')
- grad_out: float32 [1024, 1024], P('dp', 'mp')
- grad_gate: float32 [1024, 4096], P('dp', 'mp')
- grad_up: float32 [1024, 4096], P('dp', 'mp')
- grad_down: float32 [1024, 4096], P('dp', 'mp')
The draws below stay inside these ranges and needn't reach their ends.
All inputs are finite; a program needn't handle non-finite values.
Results may differ from the reference program's by a relative error of at most 0.015.
The reference program's roundings to bfloat16 on the way count: a program that leaves them out, or rounds other values in their place, can miss the bound.
Values may be sent and summed in bfloat16 or wider, within the bound.
A program may use at most 128 MiB of HBM per device.

```python
import math
import jax
import jax.numpy as jnp
import numpy as np
from jax import lax

D = 1024
HEADS = 16
HS = 64
FF = 4096
V = 1024
TABLES = 16
ROWS = 128
COLS = 64


def draw_w_qkv(key, part):
    key_base, key_factor = jax.random.split(jax.random.fold_in(key, 11), 2)
    shape = (D, 3, HEADS * HS)
    base = jnp.clip(jax.random.normal(key_base, shape, jnp.float32), -4.0, 4.0)
    factor = jnp.exp(jax.random.uniform(key_factor, (HEADS,), jnp.float32, 0.0, math.log(16.0)))
    column_factor = jnp.repeat(factor, HS)
    ones = jnp.ones((HEADS * HS,), jnp.float32)
    scaling = jnp.stack([column_factor, ones, ones], axis=0)
    return (base * scaling[None, :, :] / math.sqrt(D)).astype(jnp.bfloat16)


def draw_embed_table(key, part):
    key_base, key_scale = jax.random.split(jax.random.fold_in(key, 23), 2)
    shape = (COLS, V, D)
    base = jnp.clip(jax.random.normal(key_base, shape, jnp.float32), -3.5, 3.5)
    scale = jnp.exp(jax.random.uniform(key_scale, (COLS,), jnp.float32, 0.0, math.log(10.0)))
    return (base * scale[:, None, None]).astype(jnp.bfloat16)


def touch_ends(array, stream_key, smallest, top_value):
    dims = array.shape
    spot = [jax.random.randint(jax.random.fold_in(stream_key, axis), (), 0, dims[axis]) for axis in range(len(dims))]
    array = array.at[tuple(spot)].set(smallest)
    longest = dims.index(max(dims))
    spot[longest] = (spot[longest] + 1) % dims[longest]
    return array.at[tuple(spot)].set(top_value)


def block_levels(own_key, dims, shards, low, top_value):
    factor_of = 1.0
    for position, blocks in shards:
        steps = jax.random.uniform(jax.random.fold_in(jax.random.fold_in(own_key, 6), position), (blocks,), jnp.float32, low / len(shards), top_value / len(shards))
        factor_of = factor_of * jnp.repeat(jnp.exp(steps), dims[position] // blocks).reshape((-1,) + (1,) * (len(dims) - 1 - position))
    return factor_of


def rank_bounds(number_of, skew):
    portions = [(1 << 20) // math.isqrt(grade ** skew) + 1 for grade in range(1, number_of + 1)]
    deviation = 1 + sum(portions) // (1 << 30)
    return np.cumsum(np.array([max(1, weight // deviation) for weight in portions]))


def ranked_ids(rng, extent, number_of, slope):
    listing = rank_bounds(number_of, slope)
    ticket = jax.random.randint(jax.random.fold_in(rng, 1), extent, 0, int(listing[number_of - 1]))
    standing = jnp.searchsorted(jnp.asarray(listing, jnp.int32), ticket, side="right")
    return jax.random.permutation(jax.random.fold_in(rng, 2), number_of)[standing].astype(jnp.int32)


def noise(rng, extent, scale, most, cuts=(), held_as=jnp.bfloat16):
    drawn = jax.random.normal(rng, extent, jnp.float32) * scale
    if len(cuts) > 0:
        drawn = block_levels(rng, extent, cuts, -0.22, 0.18) * drawn
    return jnp.clip(drawn, min=-most, max=most).astype(held_as)


def setup_inputs(seed: int = 0) -> dict:
    keys = jax.random.split(jax.random.key(seed), 14)
    return {
        "token_ids": touch_ends(ranked_ids(keys[0], (ROWS, COLS), V, 2), jax.random.fold_in(keys[0], 3), 0, V - 1).astype(jnp.int32),
        "fanout": touch_ends(jax.random.randint(keys[1], (ROWS, TABLES), 1, 17), jax.random.fold_in(keys[1], 1), 1, 16).astype(jnp.int32),
        "table_of_column": touch_ends(jax.random.randint(keys[2], (COLS,), 0, TABLES), jax.random.fold_in(keys[2], 1), 0, TABLES - 1).astype(jnp.int32),
        "embed_table": draw_embed_table(jax.random.fold_in(keys[13], 71), 0),
        "start_vector": noise(keys[4], (D,), 1.0, 6.0),
        "gain_attn": jnp.clip(1.0 + 0.15 * jax.random.normal(keys[5], (D,), jnp.float32), 0.25, 1.75).astype(jnp.bfloat16),
        "gain_mlp": jnp.clip(1.0 + 0.15 * jax.random.normal(keys[6], (D,), jnp.float32), 0.25, 1.75).astype(jnp.bfloat16),
        "gain_final": jnp.clip(1.0 + 0.15 * jax.random.normal(keys[7], (D,), jnp.float32), 0.25, 1.75).astype(jnp.bfloat16),
        "w_qkv": draw_w_qkv(jax.random.fold_in(keys[13], 71), 0),
        "w_out": noise(keys[9], (D, HEADS * HS), (HEADS * HS) ** -0.5, 0.1875, ((1, 8),)),
        "w_gate": noise(keys[10], (D, FF), D ** -0.5, 0.1875, ((1, 8),)),
        "w_up": noise(keys[11], (D, FF), D ** -0.5, 0.1875, ((1, 8),)),
        "w_down": noise(keys[12], (D, FF), FF ** -0.5, 0.09375, ((1, 8),)),
    }


EPS = 1e-05
ATTN_CAP = 50.0
LOGIT_CAP = 30.0

def rms_of(values):
    floats = values.astype(jnp.float32)
    return jnp.sqrt(lax.optimization_barrier(jnp.mean(floats * floats, axis=-1, keepdims=True)) + EPS)

def normalize(values, gain, rms):
    return (values.astype(jnp.float32) / rms * gain.astype(jnp.float32)).astype(jnp.bfloat16)

def norm_back(values, d_norm, gain, rms):
    floats = values.astype(jnp.float32)
    gains = gain.astype(jnp.float32)
    total = lax.optimization_barrier(jnp.sum(gains * d_norm * floats, axis=-1, keepdims=True))
    return gains * d_norm / rms - floats * total / (floats.shape[-1] * rms * rms * rms)

def reference(token_ids, fanout, table_of_column, embed_table, start_vector, gain_attn, gain_mlp, gain_final, w_qkv, w_out, w_gate, w_up, w_down):
    fl = jnp.float32
    row_count, col_count = token_ids.shape
    model_width = embed_table.shape[2]
    vocab_size = embed_table.shape[1]
    col_index = jnp.arange(col_count, dtype=jnp.int32)
    emb = embed_table[col_index[None, :], token_ids]
    start_rows = jnp.broadcast_to(start_vector[None, None, :], (row_count, 1, model_width))
    resid_in = jnp.concatenate([start_rows, emb[:, :-1]], axis=1)
    rms_attn = rms_of(resid_in)
    norm_attn = normalize(resid_in, gain_attn, rms_attn)
    qkv = jnp.einsum('rpd,dtx->rptx', norm_attn.astype(fl), w_qkv.astype(fl)).astype(jnp.bfloat16)
    queries = qkv[:, :, 0].reshape(row_count, col_count, HEADS, HS)
    key_rows = qkv[:, :, 1].reshape(row_count, col_count, HEADS, HS)
    value_rows = qkv[:, :, 2].reshape(row_count, col_count, HEADS, HS)
    score_raw = jnp.einsum('rqhe,rkhe->rhqk', queries.astype(fl), key_rows.astype(fl)) / math.sqrt(HS)
    score = ATTN_CAP * jnp.tanh(score_raw / ATTN_CAP)
    causal = col_index[:, None] >= col_index[None, :]
    exp_score = jnp.where(causal, jnp.exp(score), 0.0)
    attn_prob = exp_score / lax.optimization_barrier(jnp.sum(exp_score, axis=-1, keepdims=True))
    prob_b = attn_prob.astype(jnp.bfloat16)
    attn_heads = jnp.einsum('rhqk,rkhe->rqhe', prob_b.astype(fl), value_rows.astype(fl)).astype(jnp.bfloat16)
    attn_out = attn_heads.reshape(row_count, col_count, HEADS * HS)
    mixed_part = jnp.einsum('rpj,dj->rpd', attn_out.astype(fl), w_out.astype(fl))
    resid_mid = (resid_in.astype(fl) + mixed_part).astype(jnp.bfloat16)
    rms_mlp = rms_of(resid_mid)
    norm_mlp = normalize(resid_mid, gain_mlp, rms_mlp)
    gate_pre = jnp.einsum('rpd,df->rpf', norm_mlp.astype(fl), w_gate.astype(fl))
    up_proj = jnp.einsum('rpd,df->rpf', norm_mlp.astype(fl), w_up.astype(fl))
    hidden = (jax.nn.silu(gate_pre) * up_proj).astype(jnp.bfloat16)
    down_part = jnp.einsum('rpf,df->rpd', hidden.astype(fl), w_down.astype(fl))
    resid_out = (resid_mid.astype(fl) + down_part).astype(jnp.bfloat16)
    rms_final = rms_of(resid_out)
    norm_final = normalize(resid_out, gain_final, rms_final)
    width_root = math.sqrt(model_width)
    logit_raw = jnp.einsum('rcd,cvd->rcv', norm_final.astype(fl), embed_table.astype(fl)) / width_root
    capped = LOGIT_CAP * jnp.tanh(logit_raw / LOGIT_CAP)
    exp_logit = jnp.exp(capped)
    exp_total = lax.optimization_barrier(jnp.sum(exp_logit, axis=-1))
    onehot = (token_ids[:, :, None] == jnp.arange(vocab_size, dtype=jnp.int32)[None, None, :]).astype(fl)
    target_logit = lax.optimization_barrier(jnp.sum(capped * onehot, axis=-1))
    nll = jnp.log(exp_total) - target_logit
    select = table_of_column[None, :, None] == jnp.arange(TABLES, dtype=jnp.int32)[None, None, :]
    counts = lax.optimization_barrier(jnp.sum(jnp.where(select, fanout[:, None, :], 0), axis=-1)).astype(fl)
    row_scale = 1.0 / (counts * row_count)
    ratio = capped / LOGIT_CAP
    d_logit = ((exp_logit / exp_total[:, :, None] - onehot) * row_scale[:, :, None] * (1.0 - ratio * ratio)).astype(jnp.bfloat16)
    d_final = jnp.einsum('rcv,cvd->rcd', d_logit.astype(fl), embed_table.astype(fl)) / width_root
    d_out = norm_back(resid_out, d_final, gain_final, rms_final).astype(jnp.bfloat16)
    d_hidden = jnp.einsum('rpd,df->rpf', d_out.astype(fl), w_down.astype(fl))
    sigmoid_gate = jax.nn.sigmoid(gate_pre)
    d_gate = (d_hidden * up_proj * sigmoid_gate * (1.0 + gate_pre * (1.0 - sigmoid_gate))).astype(jnp.bfloat16)
    d_up = (d_hidden * gate_pre * sigmoid_gate).astype(jnp.bfloat16)
    d_norm_mlp = jnp.einsum('rpf,df->rpd', d_gate.astype(fl), w_gate.astype(fl)) + jnp.einsum('rpf,df->rpd', d_up.astype(fl), w_up.astype(fl))
    d_mid = (d_out.astype(fl) + norm_back(resid_mid, d_norm_mlp, gain_mlp, rms_mlp)).astype(jnp.bfloat16)
    d_attn = jnp.einsum('rpd,dj->rpj', d_mid.astype(fl), w_out.astype(fl)).astype(jnp.bfloat16)
    d_attn = d_attn.reshape(row_count, col_count, HEADS, HS)
    d_prob = jnp.einsum('rqhe,rkhe->rhqk', d_attn.astype(fl), value_rows.astype(fl))
    ratio_s = score / ATTN_CAP
    d_score = attn_prob * (d_prob - lax.optimization_barrier(jnp.sum(attn_prob * d_prob, axis=-1, keepdims=True)))
    d_scaled = (d_score * (1.0 - ratio_s * ratio_s) / math.sqrt(HS)).astype(jnp.bfloat16)
    d_query = jnp.einsum('rhqk,rkhe->rqhe', d_scaled.astype(fl), key_rows.astype(fl))
    d_key = jnp.einsum('rhqk,rqhe->rkhe', d_scaled.astype(fl), queries.astype(fl))
    d_value = jnp.einsum('rhqk,rqhe->rkhe', prob_b.astype(fl), d_attn.astype(fl))
    d_qkv = jnp.stack([d_query, d_key, d_value], axis=2).reshape(row_count, col_count, 3, HEADS * HS).astype(jnp.bfloat16)
    d_norm_attn = jnp.einsum('rptx,dtx->rpd', d_qkv.astype(fl), w_qkv.astype(fl))
    d_in = (d_mid.astype(fl) + norm_back(resid_in, d_norm_attn, gain_attn, rms_attn)).astype(jnp.bfloat16)
    d_embed = jnp.concatenate([d_in[:, 1:], jnp.zeros((row_count, 1, model_width), jnp.bfloat16)], axis=1)
    grad_table = jnp.einsum('rcv,rcd->cvd', d_logit.astype(fl), norm_final.astype(fl)) / width_root + jnp.einsum('rcv,rcd->cvd', onehot, d_embed.astype(fl))
    grad_qkv = jnp.einsum('rpd,rptx->dtx', norm_attn.astype(fl), d_qkv.astype(fl))
    grad_out = jnp.einsum('rpd,rpj->dj', d_mid.astype(fl), attn_out.astype(fl))
    grad_gate = jnp.einsum('rpd,rpf->df', norm_mlp.astype(fl), d_gate.astype(fl))
    grad_up = jnp.einsum('rpd,rpf->df', norm_mlp.astype(fl), d_up.astype(fl))
    grad_down = jnp.einsum('rpd,rpf->df', d_out.astype(fl), hidden.astype(fl))
    return (nll, grad_table, grad_qkv, grad_out, grad_gate, grad_up, grad_down)
```

```python
import functools
import math

import jax
import jax.numpy as jnp
from jax import lax
from jax.experimental import pallas as pl
from jax.experimental.pallas import tpu as pltpu
from jax.sharding import PartitionSpec as P

HS = 64
TABLES = 16
EPS = 1e-05
ATTN_CAP = 50.0
LOGIT_CAP = 30.0
MESH = pl.DeviceIdType.MESH
FL = jnp.float32
BF = jnp.bfloat16
LANES = 128


def rms_of(floats):
    return jnp.sqrt(jnp.mean(floats * floats, axis=-1, keepdims=True) + EPS)


def norm_back(floats, d_norm, gains):
    rms = rms_of(floats)
    total = jnp.sum(gains * d_norm * floats, axis=-1, keepdims=True)
    return gains * d_norm / rms - floats * total / (floats.shape[-1] * rms * rms * rms)


def enter(n_dp, n_mp, me_dp, me_mp, exchange):
    barrier = pltpu.get_barrier_semaphore()

    def greet(axis, me, count):
        def one(off, carry):
            pl.semaphore_signal(
                barrier, inc=1, device_id={axis: lax.rem(me + off, count)}, device_id_type=MESH
            )
            return carry

        lax.fori_loop(1, count, one, 0)

    greet("mp", me_mp, n_mp)
    if exchange:
        greet("dp", me_dp, n_dp)
    pl.semaphore_wait(barrier, n_mp - 1 + (n_dp - 1 if exchange else 0))


def scatter_sum(partial, landed, send, recv, me, n, slot_of):
    size = partial.shape[0] // n
    copies = []
    for off in range(1, n):
        peer = lax.rem(me + off, n)
        copy = pltpu.make_async_remote_copy(
            src_ref=partial.at[pl.ds(pl.multiple_of(slot_of(peer) * size, size), size)],
            dst_ref=landed.at[off],
            send_sem=send.at[off],
            recv_sem=recv.at[off],
            device_id={"mp": peer},
            device_id_type=MESH,
        )
        copy.start()
        copies.append(copy)
    total = partial[pl.ds(pl.multiple_of(slot_of(me) * size, size), size), :].astype(FL)
    for off, copy in enumerate(copies, 1):
        copy.wait_recv()
        total = total + landed[off].astype(FL)
    for copy in copies:
        copy.wait_send()
    return total


def gather_slots(shard, full, send, recv, me, n, slot):
    size = shard.shape[0]
    where = pl.ds(pl.multiple_of(slot * size, size), size)
    copies = []
    for off in range(1, n):
        copy = pltpu.make_async_remote_copy(
            src_ref=shard,
            dst_ref=full.at[where],
            send_sem=send.at[off],
            recv_sem=recv.at[off],
            device_id={"mp": lax.rem(me + off, n)},
            device_id_type=MESH,
        )
        copy.start()
        copies.append(copy)
    full[where, :] = shard[...]
    for copy in copies:
        copy.wait()


def swap_tokens(values, wide, outgo, income, send, recv, me, n, shift_out, shift_in):
    count, width = values.shape
    parts = width // LANES
    for part in range(parts):
        wide[pl.ds(part, count, stride=parts), :] = values[:, part * LANES : (part + 1) * LANES]
    outgo[...] = wide[...].reshape(count, parts, LANES).astype(BF)
    spot = lax.rem(me + shift_in, n)

    def copy_of(off):
        peer = lax.rem(me + off, n)
        return pltpu.make_async_remote_copy(
            src_ref=outgo.at[lax.rem(peer + shift_out, n)],
            dst_ref=income.at[spot],
            send_sem=send.at[off],
            recv_sem=recv.at[off],
            device_id={"dp": peer},
            device_id_type=MESH,
        )

    def start(off, carry):
        copy_of(off).start()
        return carry

    def finish(off, carry):
        copy_of(off).wait()
        return carry

    lax.fori_loop(1, n, start, 0)
    income[spot] = outgo[lax.rem(me + shift_out, n)]
    lax.fori_loop(1, n, finish, 0)
    wide[...] = income[...].astype(FL).reshape(count * parts, LANES)
    return jnp.concatenate(
        [wide[pl.ds(part, count, stride=parts), :] for part in range(parts)], axis=1
    )


def flipped(slot):
    return slot + 1 - 2 * lax.rem(slot, 2)


def same(slot):
    return slot


def own_rows(ref, slot, size):
    return ref[pl.ds(pl.multiple_of(slot * size, size), size), :].astype(FL)


def step_kernel(kind, n_dp, n_mp, *refs):
    exchange = kind in ("embed", "to_cols", "to_rows", "d_embed")
    n_in = {"embed": 2, "mid": 2, "to_cols": 2, "to_rows": 3, "d_mid": 4, "d_embed": 4}[kind]
    ins, full, scratch = refs[:n_in], refs[n_in], refs[n_in + 1 :]
    landed, shard, rs_send, rs_recv, ag_send, ag_recv = scratch[:6]
    me_dp, me_mp = lax.axis_index("dp"), lax.axis_index("mp")
    parity = lax.rem(me_mp, 2)
    size = shard.shape[0]
    enter(n_dp, n_mp, me_dp, me_mp, exchange)
    partial = ins[0]
    total = scatter_sum(
        partial, landed, rs_send, rs_recv, me_mp, n_mp, flipped if kind == "embed" else same
    )
    if kind == "embed":
        values = total
    elif kind in ("mid", "to_cols"):
        values = own_rows(ins[1], me_mp, size) + total
    elif kind == "to_rows":
        values = norm_back(
            own_rows(ins[1], me_mp, size), total / math.sqrt(shard.shape[1]), ins[2][...].astype(FL)
        )
    else:
        values = own_rows(ins[3], me_mp, size) + norm_back(
            own_rows(ins[1], me_mp, size), total, ins[2][...].astype(FL)
        )
    if exchange:
        wide, outgo, income, a2a_send, a2a_recv = scratch[6:]
        shift_in = 1 - parity if kind == "embed" else 0
        shift_out = 1 - parity if kind == "d_embed" else 0
        values = swap_tokens(
            values, wide, outgo, income, a2a_send, a2a_recv, me_dp, n_dp, shift_out, shift_in
        )
        if kind == "embed":
            first = lax.broadcasted_iota(jnp.int32, values.shape, 0) + parity == 0
            values = jnp.where(first, ins[1][...].astype(FL), values)
        if kind == "d_embed":
            keep = jnp.where((me_dp == n_dp - 1) & (parity == 0), 0.0, 1.0)
            values = values * keep
    shard[...] = values.astype(BF)
    slot = flipped(me_mp) if kind == "d_embed" else me_mp
    gather_slots(shard, full, ag_send, ag_recv, me_mp, n_mp, slot)


IDS = {"embed": 1, "mid": 2, "to_cols": 3, "to_rows": 4, "d_mid": 5, "d_embed": 6, "totals": 7}


def step(kind, n_dp, n_mp, *args):
    tokens, width = args[0].shape
    size = tokens // n_mp
    dma = pltpu.SemaphoreType.DMA
    scratch = [
        pltpu.VMEM((n_mp, size, width), BF),
        pltpu.VMEM((size, width), BF),
        dma((n_mp,)),
        dma((n_mp,)),
        dma((n_mp,)),
        dma((n_mp,)),
    ]
    if kind in ("embed", "to_cols", "to_rows", "d_embed"):
        parts = width // LANES
        scratch += [
            pltpu.VMEM((size * parts, LANES), FL),
            pltpu.VMEM((size, parts, LANES), BF),
            pltpu.VMEM((size, parts, LANES), BF),
            dma((n_dp,)),
            dma((n_dp,)),
        ]
    vmem = pl.BlockSpec(memory_space=pltpu.VMEM)
    return pl.pallas_call(
        functools.partial(step_kernel, kind, n_dp, n_mp),
        out_shape=jax.ShapeDtypeStruct((tokens, width), BF),
        in_specs=[vmem] * len(args),
        out_specs=vmem,
        scratch_shapes=scratch,
        compiler_params=pltpu.CompilerParams(collective_id=IDS[kind], has_side_effects=True),
        name="step_" + kind,
    )(*args)


def totals_kernel(n_mp, mine, out, landed, send, recv):
    me = lax.axis_index("mp")
    enter(1, n_mp, 0, me, False)
    copies = []
    for off in range(1, n_mp):
        copy = pltpu.make_async_remote_copy(
            src_ref=mine,
            dst_ref=landed.at[off],
            send_sem=send.at[off],
            recv_sem=recv.at[off],
            device_id={"mp": lax.rem(me + off, n_mp)},
            device_id_type=MESH,
        )
        copy.start()
        copies.append(copy)
    total = mine[...]
    for off, copy in enumerate(copies, 1):
        copy.wait()
        total = total + landed[off]
    out[...] = total


def totals(values, n_mp):
    vmem = pl.BlockSpec(memory_space=pltpu.VMEM)
    dma = pltpu.SemaphoreType.DMA
    return pl.pallas_call(
        functools.partial(totals_kernel, n_mp),
        out_shape=jax.ShapeDtypeStruct(values.shape, FL),
        in_specs=[vmem],
        out_specs=vmem,
        scratch_shapes=[pltpu.VMEM((n_mp, *values.shape), FL), dma((n_mp,)), dma((n_mp,))],
        compiler_params=pltpu.CompilerParams(collective_id=IDS["totals"], has_side_effects=True),
        name="step_totals",
    )(values)


def normalize(values, gain):
    floats = values.astype(FL)
    return (floats / rms_of(floats) * gain.astype(FL)).astype(BF)


def dot(spec, a, b):
    return jnp.einsum(spec, a, b, preferred_element_type=FL)


def local(
    token_ids,
    fanout,
    table_of_column,
    embed_table,
    start_vector,
    gain_attn,
    gain_mlp,
    gain_final,
    w_qkv,
    w_out,
    w_gate,
    w_up,
    w_down,
):
    me_mp = lax.axis_index("mp")
    n_mp = lax.axis_size("mp")
    n_dp = lax.axis_size("dp")
    own_cols, vocab_part, width = embed_table.shape
    row_count = token_ids.shape[0]
    rows = row_count // n_dp
    tokens = row_count * own_cols
    col_count = own_cols * n_dp
    head_cols = w_qkv.shape[2]
    heads = head_cols // HS

    def row(vector):
        return vector.reshape(1, width)

    ids = token_ids.reshape(n_dp, rows, own_cols).transpose(1, 2, 0)
    local_ids = ids - me_mp * vocab_part
    hit = local_ids[..., None] == jnp.arange(vocab_part, dtype=jnp.int32)
    onehot = hit.astype(BF)
    picked = dot("rpkv,pvd->rpkd", onehot, embed_table).astype(BF).reshape(tokens, width)
    resid_in = step("embed", n_dp, n_mp, picked, row(start_vector))

    norm_attn = normalize(resid_in, gain_attn)
    qkv = dot("nd,dtx->ntx", norm_attn, w_qkv).astype(BF)
    split = qkv.reshape(rows, col_count, 3, heads, HS)
    queries, key_rows, value_rows = split[:, :, 0], split[:, :, 1], split[:, :, 2]
    score_raw = dot("rqhe,rkhe->rhqk", queries, key_rows) / math.sqrt(HS)
    score = ATTN_CAP * jnp.tanh(score_raw / ATTN_CAP)
    place = jnp.arange(col_count, dtype=jnp.int32)
    col_index = own_cols * (place % n_dp) + place // n_dp
    causal = col_index[:, None] >= col_index[None, :]
    exp_score = jnp.where(causal, jnp.exp(score), 0.0)
    attn_prob = exp_score / jnp.sum(exp_score, axis=-1, keepdims=True)
    prob_b = attn_prob.astype(BF)
    attn_out = dot("rhqk,rkhe->rqhe", prob_b, value_rows).astype(BF).reshape(tokens, head_cols)
    mixed = dot("nj,dj->nd", attn_out, w_out).astype(BF)
    resid_mid = step("mid", n_dp, n_mp, mixed, resid_in)

    norm_mlp = normalize(resid_mid, gain_mlp)
    gate_pre = dot("nd,df->nf", norm_mlp, w_gate)
    up_proj = dot("nd,df->nf", norm_mlp, w_up)
    hidden = (jax.nn.silu(gate_pre) * up_proj).astype(BF)
    down = dot("nf,df->nd", hidden, w_down).astype(BF)
    out_cols = step("to_cols", n_dp, n_mp, down, resid_mid)

    norm_final = normalize(out_cols, gain_final).reshape(rows, own_cols, n_dp, width)
    width_root = math.sqrt(width)
    logit_raw = dot("rpkd,pvd->rpkv", norm_final, embed_table) / width_root
    capped = LOGIT_CAP * jnp.tanh(logit_raw / LOGIT_CAP)
    exp_logit = jnp.exp(capped)
    sums = jnp.stack(
        [
            jnp.sum(exp_logit, axis=-1).reshape(tokens),
            jnp.sum(jnp.where(hit, capped, 0.0), axis=-1).reshape(tokens),
        ]
    ).reshape(2 * tokens // LANES, LANES)
    exp_total, target_logit = totals(sums, n_mp).reshape(2, rows, own_cols, n_dp)
    nll = jnp.log(exp_total) - target_logit
    select = table_of_column[None, :, None] == jnp.arange(TABLES, dtype=jnp.int32)[None, None, :]
    counts = jnp.sum(jnp.where(select, fanout[:, None, :], 0), axis=-1).astype(FL)
    row_scale = (1.0 / (counts * row_count)).reshape(n_dp, rows, own_cols).transpose(1, 2, 0)
    ratio = capped / LOGIT_CAP
    d_logit = (
        (exp_logit / exp_total[..., None] - hit.astype(FL))
        * row_scale[..., None]
        * (1.0 - ratio * ratio)
    ).astype(BF)
    d_final = dot("rpkv,pvd->rpkd", d_logit, embed_table).astype(BF).reshape(tokens, width)
    table_grad = dot("rpkv,rpkd->pvd", d_logit, norm_final) / width_root
    d_out = step("to_rows", n_dp, n_mp, d_final, out_cols, row(gain_final))

    d_hidden = dot("nd,df->nf", d_out, w_down)
    sigmoid_gate = jax.nn.sigmoid(gate_pre)
    d_gate = (d_hidden * up_proj * sigmoid_gate * (1.0 + gate_pre * (1.0 - sigmoid_gate))).astype(BF)
    d_up = (d_hidden * gate_pre * sigmoid_gate).astype(BF)
    d_norm_mlp = (dot("nf,df->nd", d_gate, w_gate) + dot("nf,df->nd", d_up, w_up)).astype(BF)
    mlp_terms = jnp.concatenate(
        [
            dot("nd,nf->df", norm_mlp, d_gate),
            dot("nd,nf->df", norm_mlp, d_up),
            dot("nd,nf->df", d_out, hidden),
        ],
        axis=1,
    )
    mlp_sum = lax.psum_scatter(mlp_terms, "dp", scatter_dimension=0, tiled=True)
    d_mid = step("d_mid", n_dp, n_mp, d_norm_mlp, resid_mid, row(gain_mlp), d_out)

    d_attn = dot("nd,dj->nj", d_mid, w_out).astype(BF).reshape(rows, col_count, heads, HS)
    d_prob = dot("rqhe,rkhe->rhqk", d_attn, value_rows)
    ratio_s = score / ATTN_CAP
    d_score = attn_prob * (d_prob - jnp.sum(attn_prob * d_prob, axis=-1, keepdims=True))
    d_scaled = (d_score * (1.0 - ratio_s * ratio_s) / math.sqrt(HS)).astype(BF)
    d_query = dot("rhqk,rkhe->rqhe", d_scaled, key_rows)
    d_key = dot("rhqk,rqhe->rkhe", d_scaled, queries)
    d_value = dot("rhqk,rqhe->rkhe", prob_b, d_attn)
    d_qkv = (
        jnp.stack([d_query, d_key, d_value], axis=2).reshape(tokens, 3, head_cols).astype(BF)
    )
    d_norm_attn = dot("ntx,dtx->nd", d_qkv, w_qkv).astype(BF)
    attn_terms = jnp.concatenate(
        [
            dot("nd,ntx->dtx", norm_attn, d_qkv).reshape(width, 3 * head_cols),
            dot("nd,nj->dj", d_mid, attn_out),
        ],
        axis=1,
    )
    attn_sum = lax.psum_scatter(attn_terms, "dp", scatter_dimension=0, tiled=True)
    d_embed = step("d_embed", n_dp, n_mp, d_norm_attn, resid_in, row(gain_attn), d_mid)
    table_grad = table_grad + dot(
        "rpkv,rpkd->pvd", onehot, d_embed.reshape(rows, own_cols, n_dp, width)
    )

    ff = w_gate.shape[1]
    qkv_width = 3 * head_cols
    return (
        nll.transpose(2, 0, 1).reshape(row_count, own_cols),
        table_grad,
        attn_sum[:, :qkv_width].reshape(attn_sum.shape[0], 3, head_cols),
        attn_sum[:, qkv_width:],
        mlp_sum[:, :ff],
        mlp_sum[:, ff : 2 * ff],
        mlp_sum[:, 2 * ff :],
    )


def solution(mesh):
    return jax.shard_map(
        local,
        mesh=mesh,
        in_specs=(
            P(None, "dp"),
            P(),
            P("dp"),
            P("dp", "mp", None),
            P(),
            P(),
            P(),
            P(),
            P(None, None, "mp"),
            P(None, "mp"),
            P(None, "mp"),
            P(None, "mp"),
            P(None, "mp"),
        ),
        out_specs=(
            P(None, "dp"),
            P("dp", "mp", None),
            P("dp", None, "mp"),
            P("dp", "mp"),
            P("dp", "mp"),
            P("dp", "mp"),
            P("dp", "mp"),
        ),
        check_vma=False,
    )
```

```python
import functools
import math
import types

import jax
import jax.numpy as jnp
from jax import lax
from jax.experimental import pallas as pl
from jax.experimental.pallas import tpu as pltpu
from jax.sharding import PartitionSpec as P

HS = 64
TABLES = 16
EPS = 1e-05
ATTN_CAP = 50.0
LOGIT_CAP = 30.0
MESH = pl.DeviceIdType.MESH
FL = jnp.float32
BF = jnp.bfloat16
LANES = 128
HBM = "_hbm"
MLP = "mlp_ring_"
ATTN = "attn_ring_"

EMBED, MID, COLS, ROWS, D_MID, D_EMBED = range(6)


def nn(a, b):
    return lax.dot_general(a, b, (((1,), (0,)), ((), ())), preferred_element_type=FL)


def nt(a, b):
    return lax.dot_general(a, b, (((1,), (1,)), ((), ())), preferred_element_type=FL)


def tn(a, b):
    return lax.dot_general(a, b, (((0,), (0,)), ((), ())), preferred_element_type=FL)


def rms_of(floats):
    return jnp.sqrt(jnp.mean(floats * floats, axis=-1, keepdims=True) + EPS)


def norm_back(floats, d_norm, gains):
    rms = rms_of(floats)
    total = jnp.sum(gains * d_norm * floats, axis=-1, keepdims=True)
    return gains * d_norm / rms - floats * total / (floats.shape[-1] * rms * rms * rms)


def block(index, size):
    return pl.ds(pl.multiple_of(index * size, size), size)


class Ring:
    def __init__(self, me, ref, prefix):
        for name, value in vars(ref).items():
            if name.startswith(prefix):
                setattr(self, name.removeprefix(prefix), value)
        self.me = me
        self.z, self.y, self.core = me // 4, lax.rem(me // 2, 2), lax.rem(me, 2)
        self.length = self.pair_out.shape[0]
        self.half = self.terms.shape[2] // 2
        self.seen = set()

    def chunk(self, off):
        return lax.rem(self.z + off, self.length)

    def copy(self, src, dst, send, recv, peer):
        return pltpu.make_async_remote_copy(
            src_ref=src,
            dst_ref=dst,
            send_sem=send,
            recv_sem=recv,
            device_id={"dp": peer},
            device_id_type=MESH,
        )

    def pair_copy(self, off):
        peer = self.me + 1 - 2 * self.core
        sems = self.pair_sems
        return self.copy(
            self.pair_out.at[off], self.pair_in.at[off], sems.at[0, off], sems.at[1, off], peer
        )

    def pair(self):
        n = self.length
        order = [off for near in range(1, n // 2) for off in (n - near, near)] + [n // 2, 0]
        for off in order:
            base = self.chunk(off) * 4
            for y in range(2):
                self.pair_out[off, y] = self.terms[base + 2 * y + 1 - self.core].astype(BF)
            self.pair_copy(off).start()

    def mine(self, off, y, side):
        if off not in self.seen:
            self.seen.add(off)
            self.pair_copy(off).wait_recv()
        cols = slice(side * self.half, (side + 1) * self.half)
        own = self.terms[self.chunk(off) * 4 + 2 * y + self.core, :, cols]
        return own + self.pair_in[off, y, :, cols].astype(FL)

    def hop(self, side, t):
        near = lax.rem(self.z + (1 if side == 0 else self.length - 1), self.length)
        return self.copy(
            self.hop_out.at[side, t],
            self.hop_in.at[side, t],
            self.hop_send.at[side, t],
            self.hop_recv.at[side, t],
            near * 4 + lax.rem(self.me, 4),
        )

    def step(self, t):
        for side in range(2):
            off = self.length - 1 - t if side == 0 else 1 + t
            if t > 0:
                self.hop(side, t - 1).wait_recv()
            for y in range(2):
                value = self.mine(off, y, side)
                if t > 0:
                    value = value + self.hop_in[side, t - 1, y].astype(FL)
                self.hop_out[side, t, y] = value.astype(BF)
            self.hop(side, t).start()

    def y_copy(self):
        peer = self.me + 2 - 4 * self.y
        return self.copy(self.y_out, self.y_in, self.y_sems.at[0], self.y_sems.at[1], peer)

    def cross(self):
        t = self.length - 2
        for side in range(2):
            self.hop(side, t).wait_recv()
            cols = slice(side * self.half, (side + 1) * self.half)
            for y in range(2):
                self.last[y, :, cols] = self.mine(0, y, side) + self.hop_in[side, t, y].astype(FL)
        self.y_out[...] = self.last[1 - self.y].astype(BF)
        self.y_copy().start()

    def result(self):
        self.y_copy().wait_recv()
        return self.last[self.y] + self.y_in[...].astype(FL)

    def drain(self):
        for off in range(self.length):
            self.pair_copy(off).wait_send()
        for side in range(2):
            for t in range(self.length - 1):
                self.hop(side, t).wait_send()
        self.y_copy().wait_send()


def window_kernel(n_dp, n_mp, names, *refs):
    ref = types.SimpleNamespace(**dict(zip(names, refs)))
    me_dp, me_mp = lax.axis_index("dp"), lax.axis_index("mp")
    parity, row = lax.rem(me_mp, 2), me_mp // 2
    part, land, full = ref.part, ref.land, ref.full
    tokens, width = part.shape[1:]
    size = tokens // n_mp
    half = tokens // 2
    parts = width // LANES
    root = math.sqrt(width)
    group_rows = n_mp // 2

    loads = types.SimpleNamespace()
    for slot, name in enumerate(name for name in names if name.endswith(HBM)):
        here = name.removesuffix(HBM)
        copy = pltpu.make_async_copy(getattr(ref, name), getattr(ref, here), ref.load_sem.at[slot])
        copy.start()
        setattr(loads, here, copy)

    barrier = pltpu.get_barrier_semaphore()
    for axis, me, count in (("mp", me_mp, n_mp), ("dp", me_dp, n_dp)):

        def greet(off, carry, axis=axis, me=me, count=count):
            pl.semaphore_signal(
                barrier, inc=1, device_id={axis: lax.rem(me + off, count)}, device_id_type=MESH
            )
            return carry

        lax.fori_loop(1, count, greet, 0)

    def row_slot(mp):
        return mp

    def col_slot(mp):
        return lax.rem(mp, 2) * group_rows + mp // 2

    def other_col_slot(mp):
        return (1 - lax.rem(mp, 2)) * group_rows + mp // 2

    offsets = [off for _, off in sorted((-min(off, n_mp - off), off) for off in range(1, n_mp))]

    def rs_copy(stage, off, slot_of):
        peer = lax.rem(me_mp + off, n_mp)
        return pltpu.make_async_remote_copy(
            src_ref=part.at[stage, block(slot_of(peer), size)],
            dst_ref=land.at[stage, off],
            send_sem=ref.rs_send.at[stage],
            recv_sem=ref.rs_recv.at[stage, off],
            device_id={"mp": peer},
            device_id_type=MESH,
        )

    def rs_start(stage, slot_of):
        for off in offsets:
            rs_copy(stage, off, slot_of).start()

    def rs_finish(stage, slot_of):
        total = part[stage, block(slot_of(me_mp), size), :].astype(FL)
        for off in reversed(offsets):
            rs_copy(stage, off, slot_of).wait_recv()
            total = total + land[stage, off].astype(FL)
        return total

    def ag_copy(stage, off, slot):
        where = full.at[stage, block(slot, size)]
        return pltpu.make_async_remote_copy(
            src_ref=where,
            dst_ref=where,
            send_sem=ref.ag_send.at[stage],
            recv_sem=ref.ag_recv.at[stage, off],
            device_id={"mp": lax.rem(me_mp + off, n_mp)},
            device_id_type=MESH,
        )

    def ag_start(stage, slot, values):
        full[stage, block(slot, size), :] = values.astype(BF)
        for off in offsets:
            ag_copy(stage, off, slot).start()

    def ag_finish(stage, slot):
        for off in offsets:
            ag_copy(stage, off, slot).wait_recv()

    wide, outgo, income = ref.wide, ref.outgo, ref.income

    def a2a_copy(which, off, shift_out, shift_in):
        peer = lax.rem(me_dp + off, n_dp)
        return pltpu.make_async_remote_copy(
            src_ref=outgo.at[which, lax.rem(peer + shift_out, n_dp)],
            dst_ref=income.at[which, lax.rem(me_dp + shift_in, n_dp)],
            send_sem=ref.a2a_send.at[which],
            recv_sem=ref.a2a_recv.at[which],
            device_id={"dp": peer},
            device_id_type=MESH,
        )

    def a2a_all(which):
        return pltpu.make_async_remote_copy(
            src_ref=outgo.at[which, pl.ds(0, n_dp - 1)],
            dst_ref=income.at[which, pl.ds(0, n_dp - 1)],
            send_sem=ref.a2a_send.at[which],
            recv_sem=ref.a2a_recv.at[which],
            device_id={"dp": lax.rem(me_dp + 1, n_dp)},
            device_id_type=MESH,
        )

    def a2a_start(which, values, shift_out, shift_in):
        for i in range(parts):
            wide[pl.ds(i, size, stride=parts), :] = values[:, i * LANES : (i + 1) * LANES]
        outgo[which] = wide[...].reshape(size, parts, LANES).astype(BF)

        def start(off, carry):
            a2a_copy(which, off, shift_out, shift_in).start()
            return carry

        lax.fori_loop(1, n_dp, start, 0)

    def a2a_finish(which, shift_out, shift_in):
        a2a_all(which).wait_recv()
        income[which, lax.rem(me_dp + shift_in, n_dp)] = outgo[
            which, lax.rem(me_dp + shift_out, n_dp)
        ]
        wide[...] = income[which].astype(FL).reshape(size * parts, LANES)
        return jnp.concatenate(
            [wide[pl.ds(i, size, stride=parts), :] for i in range(parts)], axis=1
        )

    def own(stage, slot):
        return full[stage, block(slot, size), :].astype(FL)

    def normalize(stage, gain, out):
        @pl.loop(0, n_mp)
        def _(i):
            floats = full[stage, block(i, size), :].astype(FL)
            out[block(i, size), :] = (floats / rms_of(floats) * gain[...].astype(FL)).astype(BF)

    def weight_terms(left, right, out, cols):
        @pl.loop(0, width // LANES)
        def _(i):
            value = tn(left[:, block(i, LANES)], right[...])
            out[pl.ds(i * 4, 4), :, cols] = value.reshape(4, LANES // 4, value.shape[1])

    vocab = lax.broadcasted_iota(jnp.int32, (LANES, half), 0)
    loads.table_in.wait()
    table_in = ref.table_in

    def hits(p):
        return vocab == ref.ids[p : p + 1, :]

    for p in range(2):
        picked = tn(hits(p).astype(FL).astype(BF), table_in[p])
        part[EMBED, p * half : (p + 1) * half, :] = picked.astype(BF)
    pl.semaphore_wait(barrier, n_mp - 1 + n_dp - 1)
    rs_start(EMBED, other_col_slot)
    a2a_start(0, rs_finish(EMBED, other_col_slot), 0, 1 - parity)
    values = a2a_finish(0, 0, 1 - parity)
    first = lax.broadcasted_iota(jnp.int32, values.shape, 0) + parity == 0
    values = jnp.where(first, ref.start[...].astype(FL), values)
    ag_start(EMBED, me_mp, values)
    ag_finish(EMBED, me_mp)

    norm_attn, qkv, attn_out = ref.norm_attn, ref.qkv, ref.attn_out
    score, prob = ref.score, ref.prob
    normalize(EMBED, ref.gain_attn, norm_attn)
    loads.w_qkv.wait()
    qkv[...] = nn(norm_attn[...], ref.w_qkv[...]).astype(BF)
    head_cols = attn_out.shape[1]
    lane = lax.broadcasted_iota(jnp.int32, (1, head_cols), 1)
    head_masks = [
        ((lane >= h * HS) & (lane < (h + 1) * HS)).astype(FL).astype(BF)
        for h in range(head_cols // HS)
    ]
    queries = qkv[:, :head_cols]
    key_rows = qkv[:, head_cols : 2 * head_cols]
    value_rows = qkv[:, 2 * head_cols :]
    cols_in_row = tokens // group_rows
    at = lax.broadcasted_iota(jnp.int32, (tokens, tokens), 0)
    to = lax.broadcasted_iota(jnp.int32, (tokens, tokens), 1)

    def column(token):
        inside = lax.rem(token, cols_in_row)
        return 2 * lax.rem(inside, n_dp) + inside // n_dp

    seen = (at // cols_in_row == to // cols_in_row) & (column(at) >= column(to))
    mixed = jnp.zeros((tokens, head_cols), FL)
    for h, mask in enumerate(head_masks):
        raw = nt(queries * mask, key_rows) / math.sqrt(HS)
        capped = ATTN_CAP * jnp.tanh(raw / ATTN_CAP)
        weights = jnp.where(seen, jnp.exp(capped), 0.0)
        weights = weights / jnp.sum(weights, axis=-1, keepdims=True)
        score[h] = capped
        prob[h] = weights
        mixed = mixed + nn(weights.astype(BF), value_rows * mask)
    attn_out[...] = mixed.astype(BF)
    loads.w_out.wait()
    part[MID] = nt(attn_out[...], ref.w_out[...]).astype(BF)
    rs_start(MID, row_slot)
    ag_start(MID, me_mp, own(EMBED, me_mp) + rs_finish(MID, row_slot))
    ag_finish(MID, me_mp)

    norm_mlp, gate_pre, up_proj, hidden = (
        ref.norm_mlp,
        ref.gate_pre,
        ref.up_proj,
        ref.hidden,
    )
    normalize(MID, ref.gain_mlp, norm_mlp)
    loads.w_gate.wait()
    gate_pre[...] = nn(norm_mlp[...], ref.w_gate[...])
    loads.w_up.wait()
    up_proj[...] = nn(norm_mlp[...], ref.w_up[...])

    @pl.loop(0, n_mp)
    def _(i):
        where = block(i, size)
        gate = gate_pre[where, :]
        hidden[where, :] = (gate * jax.nn.sigmoid(gate) * up_proj[where, :]).astype(BF)

    loads.w_down.wait()
    part[COLS] = nt(hidden[...], ref.w_down[...]).astype(BF)
    rs_start(COLS, row_slot)
    a2a_start(1, own(MID, me_mp) + rs_finish(COLS, row_slot), 0, 0)
    ag_start(COLS, col_slot(me_mp), a2a_finish(1, 0, 0))
    ag_finish(COLS, col_slot(me_mp))

    norm_final, tot, tot_in = ref.norm_final, ref.tot, ref.tot_in
    normalize(COLS, ref.gain_final, norm_final)
    tot[...] = jnp.zeros_like(tot)
    capped_of = []
    for p in range(2):
        raw = nt(table_in[p], norm_final[p * half : (p + 1) * half, :]) / root
        capped = LOGIT_CAP * jnp.tanh(raw / LOGIT_CAP)
        capped_of.append(capped)
        tot[p : p + 1, :] = jnp.sum(jnp.exp(capped), axis=0, keepdims=True)
        tot[2 + p : 3 + p, :] = jnp.sum(jnp.where(hits(p), capped, 0.0), axis=0, keepdims=True)

    def tot_copy(off):
        return pltpu.make_async_remote_copy(
            src_ref=tot,
            dst_ref=tot_in.at[off],
            send_sem=ref.tot_sems.at[0, off],
            recv_sem=ref.tot_sems.at[1, off],
            device_id={"mp": lax.rem(me_mp + off, n_mp)},
            device_id_type=MESH,
        )

    for off in offsets:
        tot_copy(off).start()
    totals = tot[...]
    for off in offsets:
        tot_copy(off).wait_recv()
        totals = totals + tot_in[off]
    ref.nll[...] = jnp.log(totals[0:2, :]) - totals[2:4, :]
    d_logits = []
    for p in range(2):
        capped = capped_of[p]
        ratio = capped / LOGIT_CAP
        d_logit = (
            (jnp.exp(capped) / totals[p : p + 1, :] - hits(p).astype(FL))
            * ref.scale[p : p + 1, :]
            * (1.0 - ratio * ratio)
        ).astype(BF)
        d_logits.append(d_logit)
        part[ROWS, p * half : (p + 1) * half, :] = tn(d_logit, table_in[p]).astype(BF)
    rs_start(ROWS, col_slot)
    for p in range(2):
        ref.table[p] = nn(d_logits[p], norm_final[p * half : (p + 1) * half, :]) / root
    d_final = rs_finish(ROWS, col_slot) / root
    d_out = norm_back(own(COLS, col_slot(me_mp)), d_final, ref.gain_final[...].astype(FL))
    a2a_start(2, d_out, 0, 0)
    ag_start(ROWS, me_mp, a2a_finish(2, 0, 0))
    ag_finish(ROWS, me_mp)

    d_hidden, d_gate_up = ref.d_hidden, ref.d_gate_up
    ff = hidden.shape[1]
    d_hidden[...] = nn(full[ROWS], ref.w_down[...])

    @pl.loop(0, n_mp)
    def _(i):
        where = block(i, size)
        gate, d_hid = gate_pre[where, :], d_hidden[where, :]
        sig = jax.nn.sigmoid(gate)
        d_gate = d_hid * up_proj[where, :] * sig * (1.0 + gate * (1.0 - sig))
        d_gate_up[where, :ff] = d_gate.astype(BF)
        d_gate_up[where, ff:] = (d_hid * gate * sig).astype(BF)

    part[D_MID] = (
        nt(d_gate_up[:, :ff], ref.w_gate[...]) + nt(d_gate_up[:, ff:], ref.w_up[...])
    ).astype(BF)
    rs_start(D_MID, row_slot)
    mlp = Ring(me_dp, ref, MLP)
    attn = Ring(me_dp, ref, ATTN)
    weight_terms(norm_mlp, d_gate_up, mlp.terms, slice(0, 2 * ff))
    weight_terms(full.at[ROWS], hidden, mlp.terms, slice(2 * ff, 3 * ff))
    mlp.pair()
    d_mid = own(ROWS, me_mp) + norm_back(
        own(MID, me_mp), rs_finish(D_MID, row_slot), ref.gain_mlp[...].astype(FL)
    )
    ag_start(D_MID, me_mp, d_mid)
    mlp.step(0)
    ag_finish(D_MID, me_mp)

    d_qkv = ref.d_qkv
    d_attn = nn(full[D_MID], ref.w_out[...]).astype(BF)
    mlp.step(1)
    d_query = jnp.zeros((tokens, head_cols), FL)
    d_key = jnp.zeros((tokens, head_cols), FL)
    d_value = jnp.zeros((tokens, head_cols), FL)
    for h, mask in enumerate(head_masks):
        weights = prob[h]
        d_attn_h = d_attn * mask
        d_prob = nt(d_attn_h, value_rows)
        ratio = score[h] / ATTN_CAP
        d_score = weights * (d_prob - jnp.sum(weights * d_prob, axis=-1, keepdims=True))
        d_scaled = (d_score * (1.0 - ratio * ratio) / math.sqrt(HS)).astype(BF)
        d_query = d_query + nn(d_scaled, key_rows * mask)
        d_key = d_key + tn(d_scaled, queries * mask)
        d_value = d_value + tn(weights.astype(BF), d_attn_h)
    d_qkv[:, :head_cols] = d_query.astype(BF)
    d_qkv[:, head_cols : 2 * head_cols] = d_key.astype(BF)
    d_qkv[:, 2 * head_cols :] = d_value.astype(BF)
    part[D_EMBED] = nt(d_qkv[...], ref.w_qkv[...]).astype(BF)
    rs_start(D_EMBED, row_slot)
    weight_terms(norm_attn, d_qkv, attn.terms, slice(0, 3 * head_cols))
    weight_terms(full.at[D_MID], attn_out, attn.terms, slice(3 * head_cols, 4 * head_cols))
    attn.pair()
    mlp.step(2)
    attn.step(0)
    d_in = own(D_MID, me_mp) + norm_back(
        own(EMBED, me_mp), rs_finish(D_EMBED, row_slot), ref.gain_attn[...].astype(FL)
    )
    a2a_start(3, d_in, 1 - parity, 0)
    mlp.step(3)
    attn.step(1)
    d_embed = a2a_finish(3, 1 - parity, 0)
    keep = jnp.where((me_dp == n_dp - 1) & (parity == 0), 0.0, 1.0)
    ag_start(D_EMBED, other_col_slot(me_mp), d_embed * keep)
    mlp.step(4)
    attn.step(2)
    mlp.step(5)
    attn.step(3)
    ag_finish(D_EMBED, other_col_slot(me_mp))
    for p in range(2):
        ref.table[p] = ref.table[p] + nn(
            hits(p).astype(FL).astype(BF), full[D_EMBED, p * half : (p + 1) * half, :]
        )
    mlp.step(6)
    attn.step(4)
    mlp.cross()
    attn.step(5)
    attn.step(6)
    ref.mlp_sum[...] = mlp.result()
    attn.cross()
    ref.attn_sum[...] = attn.result()

    for stage in range(6):
        sent = part.at[stage, pl.ds(0, (n_mp - 1) * size)]
        for sem in (ref.rs_send, ref.ag_send):
            pltpu.make_async_remote_copy(
                src_ref=sent,
                dst_ref=sent,
                send_sem=sem.at[stage],
                recv_sem=ref.rs_recv.at[stage, 0],
                device_id={"mp": lax.rem(me_mp + 1, n_mp)},
                device_id_type=MESH,
            ).wait_send()
    for which in range(4):
        a2a_all(which).wait_send()
    for off in offsets:
        tot_copy(off).wait_send()
    mlp.drain()
    attn.drain()


def ring_scratch(prefix, n_dp, width, columns):
    dma = pltpu.SemaphoreType.DMA
    length = n_dp // 4
    rows = width // n_dp
    sizes = dict(
        terms=pltpu.VMEM((n_dp, rows, columns), FL),
        pair_out=pltpu.VMEM((length, 2, rows, columns), BF),
        pair_in=pltpu.VMEM((length, 2, rows, columns), BF),
        hop_out=pltpu.VMEM((2, length - 1, 2, rows, columns // 2), BF),
        hop_in=pltpu.VMEM((2, length - 1, 2, rows, columns // 2), BF),
        last=pltpu.VMEM((2, rows, columns), FL),
        y_out=pltpu.VMEM((rows, columns), BF),
        y_in=pltpu.VMEM((rows, columns), BF),
        pair_sems=dma((2, length)),
        hop_send=dma((2, length - 1)),
        hop_recv=dma((2, length - 1)),
        y_sems=dma((2,)),
    )
    return {prefix + name: value for name, value in sizes.items()}


def local(
    token_ids,
    fanout,
    table_of_column,
    embed_table,
    start_vector,
    gain_attn,
    gain_mlp,
    gain_final,
    w_qkv,
    w_out,
    w_gate,
    w_up,
    w_down,
):
    me_mp = lax.axis_index("mp")
    n_mp = lax.axis_size("mp")
    n_dp = lax.axis_size("dp")
    own_cols, vocab_part, width = embed_table.shape
    row_count = token_ids.shape[0]
    rows = row_count // n_dp
    tokens = row_count * own_cols
    head_cols = w_qkv.shape[2]
    heads = head_cols // HS
    ff = w_gate.shape[1]
    size = tokens // n_mp
    parts = width // LANES
    dma = pltpu.SemaphoreType.DMA

    def by_column(values):
        return values.reshape(n_dp, rows, own_cols).transpose(2, 1, 0).reshape(own_cols, row_count)

    ids = by_column(token_ids) - me_mp * vocab_part
    select = table_of_column[None, :, None] == jnp.arange(TABLES, dtype=jnp.int32)[None, None, :]
    counts = jnp.sum(jnp.where(select, fanout[:, None, :], 0), axis=-1).astype(FL)
    scale = by_column(1.0 / (counts * row_count))

    whole = dict(
        ids=ids,
        scale=scale,
        start=start_vector.reshape(1, width),
        gain_attn=gain_attn.reshape(1, width),
        gain_mlp=gain_mlp.reshape(1, width),
        gain_final=gain_final.reshape(1, width),
    )
    stay = dict(
        table_in_hbm=embed_table,
        w_qkv_hbm=w_qkv.reshape(width, 3 * head_cols),
        w_out_hbm=w_out,
        w_gate_hbm=w_gate,
        w_up_hbm=w_up,
        w_down_hbm=w_down,
    )
    outs = dict(
        nll=jax.ShapeDtypeStruct((own_cols, row_count), FL),
        table=jax.ShapeDtypeStruct(embed_table.shape, FL),
        attn_sum=jax.ShapeDtypeStruct((width // n_dp, 4 * head_cols), FL),
        mlp_sum=jax.ShapeDtypeStruct((width // n_dp, 3 * ff), FL),
    )
    scratch = {name.removesuffix(HBM): pltpu.VMEM(array.shape, BF) for name, array in stay.items()}
    scratch |= dict(
        load_sem=dma((len(stay),)),
        part=pltpu.VMEM((6, tokens, width), BF),
        land=pltpu.VMEM((6, n_mp, size, width), BF),
        full=pltpu.VMEM((6, tokens, width), BF),
        rs_send=dma((6,)),
        rs_recv=dma((6, n_mp)),
        ag_send=dma((6,)),
        ag_recv=dma((6, n_mp)),
        wide=pltpu.VMEM((size * parts, LANES), FL),
        outgo=pltpu.VMEM((4, size, parts, LANES), BF),
        income=pltpu.VMEM((4, size, parts, LANES), BF),
        a2a_send=dma((4,)),
        a2a_recv=dma((4,)),
        norm_attn=pltpu.VMEM((tokens, width), BF),
        norm_mlp=pltpu.VMEM((tokens, width), BF),
        norm_final=pltpu.VMEM((tokens, width), BF),
        qkv=pltpu.VMEM((tokens, 3 * head_cols), BF),
        d_qkv=pltpu.VMEM((tokens, 3 * head_cols), BF),
        attn_out=pltpu.VMEM((tokens, head_cols), BF),
        score=pltpu.VMEM((heads, tokens, tokens), FL),
        prob=pltpu.VMEM((heads, tokens, tokens), FL),
        gate_pre=pltpu.VMEM((tokens, ff), FL),
        up_proj=pltpu.VMEM((tokens, ff), FL),
        d_hidden=pltpu.VMEM((tokens, ff), FL),
        hidden=pltpu.VMEM((tokens, ff), BF),
        d_gate_up=pltpu.VMEM((tokens, 2 * ff), BF),
        tot=pltpu.VMEM((8, LANES), FL),
        tot_in=pltpu.VMEM((n_mp, 8, LANES), FL),
        tot_sems=dma((2, n_mp)),
    )
    scratch |= ring_scratch(MLP, n_dp, width, 3 * ff)
    scratch |= ring_scratch(ATTN, n_dp, width, 4 * head_cols)
    vmem = pl.BlockSpec(memory_space=pltpu.VMEM)
    names = (*whole, *stay, *outs, *scratch)
    nll, table_grad, attn_sum, mlp_sum = pl.pallas_call(
        functools.partial(window_kernel, n_dp, n_mp, names),
        out_shape=tuple(outs.values()),
        in_specs=[vmem] * len(whole) + [pl.BlockSpec(memory_space=pl.ANY)] * len(stay),
        out_specs=(vmem,) * len(outs),
        scratch_shapes=list(scratch.values()),
        compiler_params=pltpu.CompilerParams(
            collective_id=1, has_side_effects=True, vmem_limit_bytes=63_000_000
        ),
        name="window",
    )(*whole.values(), *stay.values())
    qkv_width = 3 * head_cols
    return (
        nll.reshape(own_cols, rows, n_dp).transpose(2, 1, 0).reshape(row_count, own_cols),
        table_grad,
        attn_sum[:, :qkv_width].reshape(attn_sum.shape[0], 3, head_cols),
        attn_sum[:, qkv_width:],
        mlp_sum[:, :ff],
        mlp_sum[:, ff : 2 * ff],
        mlp_sum[:, 2 * ff :],
    )


def solution(mesh):
    return jax.shard_map(
        local,
        mesh=mesh,
        in_specs=(
            P(None, "dp"),
            P(),
            P("dp"),
            P("dp", "mp", None),
            P(),
            P(),
            P(),
            P(),
            P(None, None, "mp"),
            P(None, "mp"),
            P(None, "mp"),
            P(None, "mp"),
            P(None, "mp"),
        ),
        out_specs=(
            P(None, "dp"),
            P("dp", "mp", None),
            P("dp", None, "mp"),
            P("dp", "mp"),
            P("dp", "mp"),
            P("dp", "mp"),
            P("dp", "mp"),
        ),
        check_vma=False,
    )
```

```python
import functools
import math
import types

import jax
import jax.numpy as jnp
from jax import lax
from jax.experimental import pallas as pl
from jax.experimental.pallas import tpu as pltpu
from jax.sharding import PartitionSpec as P

HS = 64
TABLES = 16
EPS = 1e-05
ATTN_CAP = 50.0
LOGIT_CAP = 30.0
MESH = pl.DeviceIdType.MESH
FL = jnp.float32
BF = jnp.bfloat16
LANES = 128
HBM = "_hbm"
MLP = "mlp_ring_"
ATTN = "attn_ring_"

EMBED, MID, COLS, ROWS, D_MID, D_EMBED = range(6)


def nn(a, b):
    return lax.dot_general(a, b, (((1,), (0,)), ((), ())), preferred_element_type=FL)


def nt(a, b):
    return lax.dot_general(a, b, (((1,), (1,)), ((), ())), preferred_element_type=FL)


def tn(a, b):
    return lax.dot_general(a, b, (((0,), (0,)), ((), ())), preferred_element_type=FL)


def rms_of(floats):
    return jnp.sqrt(jnp.mean(floats * floats, axis=-1, keepdims=True) + EPS)


def norm_back(floats, d_norm, gains):
    rms = rms_of(floats)
    total = jnp.sum(gains * d_norm * floats, axis=-1, keepdims=True)
    return gains * d_norm / rms - floats * total / (floats.shape[-1] * rms * rms * rms)


def block(index, size):
    return pl.ds(pl.multiple_of(index * size, size), size)


class Ring:
    def __init__(self, me, ref, prefix):
        for name, value in vars(ref).items():
            if name.startswith(prefix):
                setattr(self, name.removeprefix(prefix), value)
        self.me = me
        self.z, self.y, self.core = me // 4, lax.rem(me // 2, 2), lax.rem(me, 2)
        self.length = self.pair_out.shape[0]
        self.half = self.terms.shape[2] // 2
        self.seen = set()

    def chunk(self, off):
        return lax.rem(self.z + off, self.length)

    def copy(self, src, dst, send, recv, peer):
        return pltpu.make_async_remote_copy(
            src_ref=src,
            dst_ref=dst,
            send_sem=send,
            recv_sem=recv,
            device_id={"dp": peer},
            device_id_type=MESH,
        )

    def pair_copy(self, off):
        peer = self.me + 1 - 2 * self.core
        sems = self.pair_sems
        return self.copy(
            self.pair_out.at[off], self.pair_in.at[off], sems.at[0, off], sems.at[1, off], peer
        )

    def pair(self):
        n = self.length
        order = [off for near in range(1, n // 2) for off in (n - near, near)] + [n // 2, 0]
        for off in order:
            base = self.chunk(off) * 4
            for y in range(2):
                self.pair_out[off, y] = self.terms[base + 2 * y + 1 - self.core].astype(BF)
            self.pair_copy(off).start()

    def mine(self, off, y, side):
        if off not in self.seen:
            self.seen.add(off)
            self.pair_copy(off).wait_recv()
        cols = slice(side * self.half, (side + 1) * self.half)
        own = self.terms[self.chunk(off) * 4 + 2 * y + self.core, :, cols]
        return own + self.pair_in[off, y, :, cols].astype(FL)

    def hop(self, side, t):
        near = lax.rem(self.z + (1 if side == 0 else self.length - 1), self.length)
        return self.copy(
            self.hop_out.at[side, t],
            self.hop_in.at[side, t],
            self.hop_send.at[side, t],
            self.hop_recv.at[side, t],
            near * 4 + lax.rem(self.me, 4),
        )

    def step(self, t):
        for side in range(2):
            off = self.length - 1 - t if side == 0 else 1 + t
            if t > 0:
                self.hop(side, t - 1).wait_recv()
            for y in range(2):
                value = self.mine(off, y, side)
                if t > 0:
                    value = value + self.hop_in[side, t - 1, y].astype(FL)
                self.hop_out[side, t, y] = value.astype(BF)
            self.hop(side, t).start()

    def y_copy(self):
        peer = self.me + 2 - 4 * self.y
        return self.copy(self.y_out, self.y_in, self.y_sems.at[0], self.y_sems.at[1], peer)

    def cross(self):
        t = self.length - 2
        for side in range(2):
            self.hop(side, t).wait_recv()
            cols = slice(side * self.half, (side + 1) * self.half)
            for y in range(2):
                self.last[y, :, cols] = self.mine(0, y, side) + self.hop_in[side, t, y].astype(FL)
        self.y_out[...] = self.last[1 - self.y].astype(BF)
        self.y_copy().start()

    def result(self):
        self.y_copy().wait_recv()
        return self.last[self.y] + self.y_in[...].astype(FL)

    def drain(self):
        for off in range(self.length):
            self.pair_copy(off).wait_send()
        for side in range(2):
            for t in range(self.length - 1):
                self.hop(side, t).wait_send()
        self.y_copy().wait_send()


def window_kernel(n_dp, n_mp, names, *refs):
    ref = types.SimpleNamespace(**dict(zip(names, refs)))
    me_dp, me_mp = lax.axis_index("dp"), lax.axis_index("mp")
    parity, row = lax.rem(me_mp, 2), me_mp // 2
    part, land, full = ref.part, ref.land, ref.full
    tokens, width = part.shape[1:]
    size = tokens // n_mp
    half = tokens // 2
    parts = width // LANES
    root = math.sqrt(width)
    group_rows = n_mp // 2

    loads = types.SimpleNamespace()
    for slot, name in enumerate(name for name in names if name.endswith(HBM)):
        here = name.removesuffix(HBM)
        if here == "w_qkv":
            continue
        copy = pltpu.make_async_copy(getattr(ref, name), getattr(ref, here), ref.load_sem.at[slot])
        copy.start()
        setattr(loads, here, copy)
    head_width = ref.attn_out.shape[1]
    qkv_loads = [
        pltpu.make_async_copy(
            ref.w_qkv_hbm.at[t],
            ref.w_qkv.at[:, t * head_width : (t + 1) * head_width],
            ref.qkv_sem.at[t],
        )
        for t in range(3)
    ]
    for copy in qkv_loads:
        copy.start()

    barrier = pltpu.get_barrier_semaphore()
    for axis, me, count in (("mp", me_mp, n_mp), ("dp", me_dp, n_dp)):

        def greet(off, carry, axis=axis, me=me, count=count):
            pl.semaphore_signal(
                barrier, inc=1, device_id={axis: lax.rem(me + off, count)}, device_id_type=MESH
            )
            return carry

        lax.fori_loop(1, count, greet, 0)

    def row_slot(mp):
        return mp

    def col_slot(mp):
        return lax.rem(mp, 2) * group_rows + mp // 2

    def other_col_slot(mp):
        return (1 - lax.rem(mp, 2)) * group_rows + mp // 2

    offsets = [off for _, off in sorted((-min(off, n_mp - off), off) for off in range(1, n_mp))]

    def rs_copy(stage, off, slot_of):
        peer = lax.rem(me_mp + off, n_mp)
        return pltpu.make_async_remote_copy(
            src_ref=part.at[stage, block(slot_of(peer), size)],
            dst_ref=land.at[stage, off],
            send_sem=ref.rs_send.at[stage],
            recv_sem=ref.rs_recv.at[stage, off],
            device_id={"mp": peer},
            device_id_type=MESH,
        )

    def rs_start(stage, slot_of):
        for off in offsets:
            rs_copy(stage, off, slot_of).start()

    def rs_finish(stage, slot_of):
        total = part[stage, block(slot_of(me_mp), size), :].astype(FL)
        for off in reversed(offsets):
            rs_copy(stage, off, slot_of).wait_recv()
            total = total + land[stage, off].astype(FL)
        return total

    ring = n_mp // 2
    m_x, m_y = me_mp // 2, lax.rem(me_mp, 2)

    def place(dx, dy):
        return 2 * lax.rem(m_x + dx, ring) + (1 - m_y if dy else m_y)

    def ag_copy(stage, channel, origin, peer, slot_of, rows=(0, 2)):
        start, stop = rows
        piece = size // 2
        first_row = pl.multiple_of(slot_of(origin) * size + start * piece, piece)
        where = full.at[stage, pl.ds(first_row, (stop - start) * piece)]
        return pltpu.make_async_remote_copy(
            src_ref=where,
            dst_ref=where,
            send_sem=ref.ag_send.at[stage],
            recv_sem=ref.ag_recv.at[stage, channel],
            device_id={"mp": peer},
            device_id_type=MESH,
        )

    up, down, far = 1, ring - 1, ring // 2

    def ag_start(stage, slot_of, values):
        full[stage, block(slot_of(me_mp), size), :] = values.astype(BF)
        ag_copy(stage, 0, me_mp, place(0, 1), slot_of).start()
        ag_copy(stage, 1, me_mp, place(up, 0), slot_of).start()
        ag_copy(stage, 2, me_mp, place(down, 0), slot_of).start()

    def ag_got(stage, channel, origin, slot_of, rows=(0, 2)):
        ag_copy(stage, channel, origin, place(0, 1), slot_of, rows).wait_recv()

    def ag_finish(stage, slot_of):
        twin = place(0, 1)
        ag_got(stage, 0, twin, slot_of)
        ag_copy(stage, 3, twin, place(up, 0), slot_of).start()
        ag_copy(stage, 4, twin, place(down, 0), slot_of).start()
        ag_got(stage, 1, place(down, 0), slot_of)
        ag_copy(stage, 5, place(down, 0), place(up, 0), slot_of, (0, 1)).start()
        ag_got(stage, 2, place(up, 0), slot_of)
        ag_copy(stage, 6, place(up, 0), place(down, 0), slot_of, (1, 2)).start()
        ag_got(stage, 5, place(far, 0), slot_of, (0, 1))
        ag_got(stage, 6, place(far, 0), slot_of, (1, 2))
        ag_copy(stage, 7, place(far, 0), twin, slot_of).start()
        ag_got(stage, 3, place(down, 1), slot_of)
        ag_got(stage, 4, place(up, 1), slot_of)
        ag_got(stage, 7, place(far, 1), slot_of)

    wide, outgo, income = ref.wide, ref.outgo, ref.income

    def a2a_copy(which, off, shift_out, shift_in):
        peer = lax.rem(me_dp + off, n_dp)
        return pltpu.make_async_remote_copy(
            src_ref=outgo.at[which, lax.rem(peer + shift_out, n_dp)],
            dst_ref=income.at[which, lax.rem(me_dp + shift_in, n_dp)],
            send_sem=ref.a2a_send.at[which],
            recv_sem=ref.a2a_recv.at[which],
            device_id={"dp": peer},
            device_id_type=MESH,
        )

    def a2a_all(which):
        return pltpu.make_async_remote_copy(
            src_ref=outgo.at[which, pl.ds(0, n_dp - 1)],
            dst_ref=income.at[which, pl.ds(0, n_dp - 1)],
            send_sem=ref.a2a_send.at[which],
            recv_sem=ref.a2a_recv.at[which],
            device_id={"dp": lax.rem(me_dp + 1, n_dp)},
            device_id_type=MESH,
        )

    def a2a_start(which, values, shift_out, shift_in):
        for i in range(parts):
            wide[pl.ds(i, size, stride=parts), :] = values[:, i * LANES : (i + 1) * LANES]
        outgo[which] = wide[...].reshape(size, parts, LANES).astype(BF)

        def start(off, carry):
            a2a_copy(which, off, shift_out, shift_in).start()
            return carry

        lax.fori_loop(1, n_dp, start, 0)

    def a2a_finish(which, shift_out, shift_in):
        a2a_all(which).wait_recv()
        income[which, lax.rem(me_dp + shift_in, n_dp)] = outgo[
            which, lax.rem(me_dp + shift_out, n_dp)
        ]
        wide[...] = income[which].astype(FL).reshape(size * parts, LANES)
        return jnp.concatenate(
            [wide[pl.ds(i, size, stride=parts), :] for i in range(parts)], axis=1
        )

    def own(stage, slot):
        return full[stage, block(slot, size), :].astype(FL)

    def normalize(stage, gain, out):
        @pl.loop(0, n_mp)
        def _(i):
            floats = full[stage, block(i, size), :].astype(FL)
            out[block(i, size), :] = (floats / rms_of(floats) * ref.vectors[gain : gain + 1, :]).astype(BF)

    def weight_terms(left, right, out, cols):
        @pl.loop(0, width // LANES)
        def _(i):
            value = tn(left[:, block(i, LANES)], right[...])
            out[pl.ds(i * 4, 4), :, cols] = value.reshape(4, LANES // 4, value.shape[1])

    vocab = lax.broadcasted_iota(jnp.int32, (LANES, half), 0)
    loads.table_in.wait()
    table_in = ref.table_in

    def hits(p):
        return vocab == ref.ids[p : p + 1, :]

    for p in range(2):
        picked = tn(hits(p).astype(FL).astype(BF), table_in[p])
        part[EMBED, p * half : (p + 1) * half, :] = picked.astype(BF)
    pl.semaphore_wait(barrier, n_mp - 1 + n_dp - 1)
    rs_start(EMBED, other_col_slot)
    a2a_start(0, rs_finish(EMBED, other_col_slot), 0, 1 - parity)
    values = a2a_finish(0, 0, 1 - parity)
    first = lax.broadcasted_iota(jnp.int32, values.shape, 0) + parity == 0
    values = jnp.where(first, ref.vectors[0:1, :], values)
    ag_start(EMBED, row_slot, values)
    ag_finish(EMBED, row_slot)

    norm_attn, qkv, attn_out = ref.norm_attn, ref.qkv, ref.attn_out
    score, prob = ref.score, ref.prob
    normalize(EMBED, 1, norm_attn)
    for copy in qkv_loads:
        copy.wait()
    qkv[...] = nn(norm_attn[...], ref.w_qkv[...]).astype(BF)
    head_cols = attn_out.shape[1]
    lane = lax.broadcasted_iota(jnp.int32, (1, head_cols), 1)
    head_masks = [
        ((lane >= h * HS) & (lane < (h + 1) * HS)).astype(FL).astype(BF)
        for h in range(head_cols // HS)
    ]
    queries = qkv[:, :head_cols]
    key_rows = qkv[:, head_cols : 2 * head_cols]
    value_rows = qkv[:, 2 * head_cols :]
    cols_in_row = tokens // group_rows
    at = lax.broadcasted_iota(jnp.int32, (tokens, tokens), 0)
    to = lax.broadcasted_iota(jnp.int32, (tokens, tokens), 1)

    def column(token):
        inside = lax.rem(token, cols_in_row)
        return 2 * lax.rem(inside, n_dp) + inside // n_dp

    seen = (at // cols_in_row == to // cols_in_row) & (column(at) >= column(to))
    mixed = jnp.zeros((tokens, head_cols), FL)
    for h, mask in enumerate(head_masks):
        raw = nt(queries * mask, key_rows) / math.sqrt(HS)
        capped = ATTN_CAP * jnp.tanh(raw / ATTN_CAP)
        weights = jnp.where(seen, jnp.exp(capped), 0.0)
        weights = weights / jnp.sum(weights, axis=-1, keepdims=True)
        score[h] = capped
        prob[h] = weights
        mixed = mixed + nn(weights.astype(BF), value_rows * mask)
    attn_out[...] = mixed.astype(BF)
    loads.w_out.wait()
    part[MID] = nt(attn_out[...], ref.w_out[...]).astype(BF)
    rs_start(MID, row_slot)
    ag_start(MID, row_slot, own(EMBED, me_mp) + rs_finish(MID, row_slot))
    ag_finish(MID, row_slot)

    norm_mlp, gate_pre, up_proj, hidden = (
        ref.norm_mlp,
        ref.gate_pre,
        ref.up_proj,
        ref.hidden,
    )
    normalize(MID, 2, norm_mlp)
    loads.w_gate.wait()
    gate_pre[...] = nn(norm_mlp[...], ref.w_gate[...])
    loads.w_up.wait()
    up_proj[...] = nn(norm_mlp[...], ref.w_up[...])

    @pl.loop(0, n_mp)
    def _(i):
        where = block(i, size)
        gate = gate_pre[where, :]
        hidden[where, :] = (gate * jax.nn.sigmoid(gate) * up_proj[where, :]).astype(BF)

    loads.w_down.wait()
    part[COLS] = nt(hidden[...], ref.w_down[...]).astype(BF)
    rs_start(COLS, row_slot)
    a2a_start(1, own(MID, me_mp) + rs_finish(COLS, row_slot), 0, 0)
    ag_start(COLS, col_slot, a2a_finish(1, 0, 0))
    ag_finish(COLS, col_slot)

    norm_final, tot, tot_in = ref.norm_final, ref.tot, ref.tot_in
    normalize(COLS, 3, norm_final)
    tot[...] = jnp.zeros_like(tot)
    capped_of = []
    for p in range(2):
        raw = nt(table_in[p], norm_final[p * half : (p + 1) * half, :]) / root
        capped = LOGIT_CAP * jnp.tanh(raw / LOGIT_CAP)
        capped_of.append(capped)
        tot[p : p + 1, :] = jnp.sum(jnp.exp(capped), axis=0, keepdims=True)
        tot[2 + p : 3 + p, :] = jnp.sum(jnp.where(hits(p), capped, 0.0), axis=0, keepdims=True)

    def tot_copy(off):
        return pltpu.make_async_remote_copy(
            src_ref=tot,
            dst_ref=tot_in.at[off],
            send_sem=ref.tot_sems.at[0, off],
            recv_sem=ref.tot_sems.at[1, off],
            device_id={"mp": lax.rem(me_mp + off, n_mp)},
            device_id_type=MESH,
        )

    for off in offsets:
        tot_copy(off).start()
    totals = tot[...]
    for off in offsets:
        tot_copy(off).wait_recv()
        totals = totals + tot_in[off]
    ref.nll[...] = jnp.log(totals[0:2, :]) - totals[2:4, :]
    d_logits = []
    for p in range(2):
        capped = capped_of[p]
        ratio = capped / LOGIT_CAP
        d_logit = (
            (jnp.exp(capped) / totals[p : p + 1, :] - hits(p).astype(FL))
            * ref.scale[p : p + 1, :]
            * (1.0 - ratio * ratio)
        ).astype(BF)
        d_logits.append(d_logit)
        part[ROWS, p * half : (p + 1) * half, :] = tn(d_logit, table_in[p]).astype(BF)
    rs_start(ROWS, col_slot)
    for p in range(2):
        ref.table[p] = nn(d_logits[p], norm_final[p * half : (p + 1) * half, :]) / root
    d_final = rs_finish(ROWS, col_slot) / root
    d_out = norm_back(own(COLS, col_slot(me_mp)), d_final, ref.vectors[3:4, :])
    a2a_start(2, d_out, 0, 0)
    ag_start(ROWS, row_slot, a2a_finish(2, 0, 0))
    ag_finish(ROWS, row_slot)

    d_hidden, d_gate_up = ref.d_hidden, ref.d_gate_up
    ff = hidden.shape[1]
    d_hidden[...] = nn(full[ROWS], ref.w_down[...])

    @pl.loop(0, n_mp)
    def _(i):
        where = block(i, size)
        gate, d_hid = gate_pre[where, :], d_hidden[where, :]
        sig = jax.nn.sigmoid(gate)
        d_gate = d_hid * up_proj[where, :] * sig * (1.0 + gate * (1.0 - sig))
        d_gate_up[where, :ff] = d_gate.astype(BF)
        d_gate_up[where, ff:] = (d_hid * gate * sig).astype(BF)

    part[D_MID] = (
        nt(d_gate_up[:, :ff], ref.w_gate[...]) + nt(d_gate_up[:, ff:], ref.w_up[...])
    ).astype(BF)
    rs_start(D_MID, row_slot)
    mlp = Ring(me_dp, ref, MLP)
    attn = Ring(me_dp, ref, ATTN)
    weight_terms(norm_mlp, d_gate_up, mlp.terms, slice(0, 2 * ff))
    weight_terms(full.at[ROWS], hidden, mlp.terms, slice(2 * ff, 3 * ff))
    mlp.pair()
    d_mid = own(ROWS, me_mp) + norm_back(
        own(MID, me_mp), rs_finish(D_MID, row_slot), ref.vectors[2:3, :]
    )
    ag_start(D_MID, row_slot, d_mid)
    mlp.step(0)
    ag_finish(D_MID, row_slot)

    d_qkv = ref.d_qkv
    d_attn = nn(full[D_MID], ref.w_out[...]).astype(BF)
    mlp.step(1)
    d_query = jnp.zeros((tokens, head_cols), FL)
    d_key = jnp.zeros((tokens, head_cols), FL)
    d_value = jnp.zeros((tokens, head_cols), FL)
    for h, mask in enumerate(head_masks):
        weights = prob[h]
        d_attn_h = d_attn * mask
        d_prob = nt(d_attn_h, value_rows)
        ratio = score[h] / ATTN_CAP
        d_score = weights * (d_prob - jnp.sum(weights * d_prob, axis=-1, keepdims=True))
        d_scaled = (d_score * (1.0 - ratio * ratio) / math.sqrt(HS)).astype(BF)
        d_query = d_query + nn(d_scaled, key_rows * mask)
        d_key = d_key + tn(d_scaled, queries * mask)
        d_value = d_value + tn(weights.astype(BF), d_attn_h)
    d_qkv[:, :head_cols] = d_query.astype(BF)
    d_qkv[:, head_cols : 2 * head_cols] = d_key.astype(BF)
    d_qkv[:, 2 * head_cols :] = d_value.astype(BF)
    part[D_EMBED] = nt(d_qkv[...], ref.w_qkv[...]).astype(BF)
    rs_start(D_EMBED, row_slot)
    weight_terms(norm_attn, d_qkv, attn.terms, slice(0, 3 * head_cols))
    weight_terms(full.at[D_MID], attn_out, attn.terms, slice(3 * head_cols, 4 * head_cols))
    attn.pair()
    mlp.step(2)
    attn.step(0)
    d_in = own(D_MID, me_mp) + norm_back(
        own(EMBED, me_mp), rs_finish(D_EMBED, row_slot), ref.vectors[1:2, :]
    )
    a2a_start(3, d_in, 1 - parity, 0)
    mlp.step(3)
    attn.step(1)
    d_embed = a2a_finish(3, 1 - parity, 0)
    keep = jnp.where((me_dp == n_dp - 1) & (parity == 0), 0.0, 1.0)
    ag_start(D_EMBED, other_col_slot, d_embed * keep)
    mlp.step(4)
    attn.step(2)
    mlp.step(5)
    attn.step(3)
    ag_finish(D_EMBED, other_col_slot)
    for p in range(2):
        ref.table[p] = ref.table[p] + nn(
            hits(p).astype(FL).astype(BF), full[D_EMBED, p * half : (p + 1) * half, :]
        )
    mlp.step(6)
    attn.step(4)
    mlp.cross()
    attn.step(5)
    attn.step(6)
    mlp_sum = mlp.result()
    for i, out in enumerate((ref.sum_gate, ref.sum_up, ref.sum_down)):
        out[...] = mlp_sum[:, i * ff : (i + 1) * ff]
    attn.cross()
    attn_sum = attn.result()
    for t in range(3):
        ref.sum_qkv[t] = attn_sum[:, t * head_cols : (t + 1) * head_cols]
    ref.sum_out[...] = attn_sum[:, 3 * head_cols :]

    for stage in range(6):
        sent = part.at[stage, pl.ds(0, (n_mp - 1) * size)]
        for sem in (ref.rs_send, ref.ag_send):
            pltpu.make_async_remote_copy(
                src_ref=sent,
                dst_ref=sent,
                send_sem=sem.at[stage],
                recv_sem=ref.rs_recv.at[stage, 0],
                device_id={"mp": lax.rem(me_mp + 1, n_mp)},
                device_id_type=MESH,
            ).wait_send()
    for which in range(4):
        a2a_all(which).wait_send()
    for off in offsets:
        tot_copy(off).wait_send()
    mlp.drain()
    attn.drain()


def ring_scratch(prefix, n_dp, width, columns):
    dma = pltpu.SemaphoreType.DMA
    length = n_dp // 4
    rows = width // n_dp
    sizes = dict(
        terms=pltpu.VMEM((n_dp, rows, columns), FL),
        pair_out=pltpu.VMEM((length, 2, rows, columns), BF),
        pair_in=pltpu.VMEM((length, 2, rows, columns), BF),
        hop_out=pltpu.VMEM((2, length - 1, 2, rows, columns // 2), BF),
        hop_in=pltpu.VMEM((2, length - 1, 2, rows, columns // 2), BF),
        last=pltpu.VMEM((2, rows, columns), FL),
        y_out=pltpu.VMEM((rows, columns), BF),
        y_in=pltpu.VMEM((rows, columns), BF),
        pair_sems=dma((2, length)),
        hop_send=dma((2, length - 1)),
        hop_recv=dma((2, length - 1)),
        y_sems=dma((2,)),
    )
    return {prefix + name: value for name, value in sizes.items()}


def local(
    token_ids,
    fanout,
    table_of_column,
    embed_table,
    start_vector,
    gain_attn,
    gain_mlp,
    gain_final,
    w_qkv,
    w_out,
    w_gate,
    w_up,
    w_down,
):
    me_mp = lax.axis_index("mp")
    n_mp = lax.axis_size("mp")
    n_dp = lax.axis_size("dp")
    own_cols, vocab_part, width = embed_table.shape
    row_count = token_ids.shape[0]
    rows = row_count // n_dp
    tokens = row_count * own_cols
    head_cols = w_qkv.shape[2]
    heads = head_cols // HS
    ff = w_gate.shape[1]
    size = tokens // n_mp
    parts = width // LANES
    dma = pltpu.SemaphoreType.DMA

    def by_column(values):
        return values.reshape(n_dp, rows, own_cols).transpose(2, 1, 0).reshape(own_cols, row_count)

    ids = by_column(token_ids) - me_mp * vocab_part
    select = table_of_column[None, :, None] == jnp.arange(TABLES, dtype=jnp.int32)[None, None, :]
    counts = jnp.sum(jnp.where(select, fanout[:, None, :], 0), axis=-1).astype(FL)
    scale = by_column(1.0 / (counts * row_count))

    whole = dict(
        ids=ids,
        scale=scale,
        vectors=jnp.stack([start_vector, gain_attn, gain_mlp, gain_final]).astype(FL),
    )
    stay = dict(
        table_in_hbm=embed_table,
        w_qkv_hbm=w_qkv.transpose(1, 0, 2),
        w_out_hbm=w_out,
        w_gate_hbm=w_gate,
        w_up_hbm=w_up,
        w_down_hbm=w_down,
    )
    outs = dict(
        nll=jax.ShapeDtypeStruct((own_cols, row_count), FL),
        table=jax.ShapeDtypeStruct(embed_table.shape, FL),
        sum_qkv=jax.ShapeDtypeStruct((3, width // n_dp, head_cols), FL),
        sum_out=jax.ShapeDtypeStruct((width // n_dp, head_cols), FL),
        sum_gate=jax.ShapeDtypeStruct((width // n_dp, ff), FL),
        sum_up=jax.ShapeDtypeStruct((width // n_dp, ff), FL),
        sum_down=jax.ShapeDtypeStruct((width // n_dp, ff), FL),
    )
    scratch = {name.removesuffix(HBM): pltpu.VMEM(array.shape, BF) for name, array in stay.items()}
    scratch |= dict(
        w_qkv=pltpu.VMEM((width, 3 * head_cols), BF),
        qkv_sem=dma((3,)),
        load_sem=dma((len(stay),)),
        part=pltpu.VMEM((6, tokens, width), BF),
        land=pltpu.VMEM((6, n_mp, size, width), BF),
        full=pltpu.VMEM((6, tokens, width), BF),
        rs_send=dma((6,)),
        rs_recv=dma((6, n_mp)),
        ag_send=dma((6,)),
        ag_recv=dma((6, n_mp)),
        wide=pltpu.VMEM((size * parts, LANES), FL),
        outgo=pltpu.VMEM((4, size, parts, LANES), BF),
        income=pltpu.VMEM((4, size, parts, LANES), BF),
        a2a_send=dma((4,)),
        a2a_recv=dma((4,)),
        norm_attn=pltpu.VMEM((tokens, width), BF),
        norm_mlp=pltpu.VMEM((tokens, width), BF),
        norm_final=pltpu.VMEM((tokens, width), BF),
        qkv=pltpu.VMEM((tokens, 3 * head_cols), BF),
        d_qkv=pltpu.VMEM((tokens, 3 * head_cols), BF),
        attn_out=pltpu.VMEM((tokens, head_cols), BF),
        score=pltpu.VMEM((heads, tokens, tokens), FL),
        prob=pltpu.VMEM((heads, tokens, tokens), FL),
        gate_pre=pltpu.VMEM((tokens, ff), FL),
        up_proj=pltpu.VMEM((tokens, ff), FL),
        d_hidden=pltpu.VMEM((tokens, ff), FL),
        hidden=pltpu.VMEM((tokens, ff), BF),
        d_gate_up=pltpu.VMEM((tokens, 2 * ff), BF),
        tot=pltpu.VMEM((8, LANES), FL),
        tot_in=pltpu.VMEM((n_mp, 8, LANES), FL),
        tot_sems=dma((2, n_mp)),
    )
    scratch |= ring_scratch(MLP, n_dp, width, 3 * ff)
    scratch |= ring_scratch(ATTN, n_dp, width, 4 * head_cols)
    vmem = pl.BlockSpec(memory_space=pltpu.VMEM)
    names = (*whole, *stay, *outs, *scratch)
    nll, table_grad, sum_qkv, *sums = pl.pallas_call(
        functools.partial(window_kernel, n_dp, n_mp, names),
        out_shape=tuple(outs.values()),
        in_specs=[vmem] * len(whole) + [pl.BlockSpec(memory_space=pl.ANY)] * len(stay),
        out_specs=(vmem,) * len(outs),
        scratch_shapes=list(scratch.values()),
        compiler_params=pltpu.CompilerParams(
            collective_id=1, has_side_effects=True, vmem_limit_bytes=63_000_000
        ),
        name="window",
    )(*whole.values(), *stay.values())
    return (
        nll.reshape(own_cols, rows, n_dp).transpose(2, 1, 0).reshape(row_count, own_cols),
        table_grad,
        sum_qkv.transpose(1, 0, 2),
        *sums,
    )


def solution(mesh):
    return jax.shard_map(
        local,
        mesh=mesh,
        in_specs=(
            P(None, "dp"),
            P(),
            P("dp"),
            P("dp", "mp", None),
            P(),
            P(),
            P(),
            P(),
            P(None, None, "mp"),
            P(None, "mp"),
            P(None, "mp"),
            P(None, "mp"),
            P(None, "mp"),
        ),
        out_specs=(
            P(None, "dp"),
            P("dp", "mp", None),
            P("dp", None, "mp"),
            P("dp", "mp"),
            P("dp", "mp"),
            P("dp", "mp"),
            P("dp", "mp"),
        ),
        check_vma=False,
    )
```
